32 devices in a mesh: seq: 8 (over z, y), head: 4 (over x, core).
Axes of the slice: x: 2, y: 2, z: 4, core: 2. Of those that a mesh axis runs over, the one named last changes fastest.
Arguments:
- block_input: bfloat16 [2, 1024, 2048], P(None, 'seq'), may hold values from -6 to 6
- pre_scales: float32 [2048], replicated, may hold values from 0.5 to 1.5
- query_weight: bfloat16 [2048, 2048], P(None, 'head'), may hold values from -0.125 to 0.125
- key_weight: bfloat16 [2048, 2048], P(None, 'head'), may hold values from -0.125 to 0.125
- value_weight: bfloat16 [2048, 3456], P(None, 'head'), may hold values from -0.125 to 0.125
- swish_weight: bfloat16 [2048, 3456], P(None, 'head'), may hold values from -0.125 to 0.125
- projection: bfloat16 [3456, 2048], P('head'), may hold values from -0.109375 to 0.109375
- mid_scales: float32 [2048], replicated, may hold values from 0.5 to 1.5
- gelu_weight: bfloat16 [2048, 3456], P(None, 'head'), may hold values from -0.125 to 0.125
- linear_weight: bfloat16 [2048, 3456], P(None, 'head'), may hold values from -0.125 to 0.125
- down_weight: bfloat16 [3456, 2048], P('head'), may hold values from -0.109375 to 0.109375
- cotangent: bfloat16 [2, 1024, 2048], P(None, 'seq'), may hold values from -6 to 6
Outputs:
- block_output: bfloat16 [2, 1024, 2048], P(None, 'seq')
- input_grad: float32 [2, 1024, 2048], P(None, 'seq')
- pre_grad: float32 [2048], P('seq')
- query_grad: float32 [2048, 2048], P('seq', 'head')
- key_grad: float32 [2048, 2048], P('seq', 'head')
- value_grad: float32 [2048, 3456], P('seq', 'head')
- swish_grad: float32 [2048, 3456], P('seq', 'head')
- projection_grad: float32 [3456, 2048], P('head', 'seq')
- mid_grad: float32 [2048], P('seq')
- gelu_grad: float32 [2048, 3456], P('seq', 'head')
- linear_grad: float32 [2048, 3456], P('seq', 'head')
- down_grad: float32 [3456, 2048], P('head', 'seq')
The draws below stay inside these ranges and needn't reach their ends.
All inputs are finite; a program needn't handle non-finite values.
Results may differ from the reference program's by a relative error of at most 0.015.
Values sent between devices are 32-bit elements; how exact they have to be, the bound alone decides.
No kernel may reach another device: no remote copies, remote signals or barrier semaphores. Data moves between devices by JAX's collectives and lax.ppermute only.
A program may use at most 256 MiB of HBM per device.

```python
import jax
import jax.numpy as jnp
from jax import lax

D = 2048
HEADS = 8
DK = 256
DV = 432
FF = 3456
SEQS = 2
BLK = 128
LEN = 1024


def spiked(array, key, source, target, shards_of, factor):
    def block_of(position):
        return (jnp.arange(array.shape[position]) // (array.shape[position] // shards_of)).reshape((-1,) + (1,) * (array.ndim - 1 - position))

    one_side = jax.random.permutation(key, shards_of)[block_of(target)]
    other_side = (block_of(target) + shards_of // 2) % shards_of
    return jnp.where((block_of(source) == one_side) | (block_of(source) == other_side), factor * array, array)


def levels(key, shape, shards, least, top_value):
    def one(axis_at, shards_of):
        steps = jax.random.uniform(jax.random.fold_in(jax.random.fold_in(key, 6), axis_at), (shards_of,), jnp.float32, least / len(shards), top_value / len(shards))
        return jnp.repeat(jnp.exp(steps), shape[axis_at] // shards_of).reshape((-1,) + (1,) * (len(shape) - axis_at - 1))

    factor_of = one(*shards[0])
    for cut in shards[1:]:
        factor_of = factor_of * one(*cut)
    return factor_of


def noise(key, dims, scale, limit, cuts=(), kind=jnp.bfloat16):
    gain = levels(key, dims, cuts, -0.22, 0.18) if cuts else 1.0
    drawn = jax.random.normal(key, dims, jnp.float32) * scale * gain
    return jnp.minimum(jnp.maximum(drawn, -limit), limit).astype(kind)


def bell_draw_with(rng, extent, deviation, limit, pieces, heavy, held_as=jnp.bfloat16):
    drawn = deviation * jax.random.normal(rng, extent, jnp.float32)
    if pieces:
        drawn = drawn * levels(rng, extent, pieces, -0.22, 0.18)
    return jnp.clip(spiked(drawn, jax.random.fold_in(rng, 3), *heavy), -limit, limit).astype(held_as)


def setup_inputs(seed: int = 0) -> dict:
    splits = jax.random.split(jax.random.key(seed), 13)
    return {
        "block_input": noise(splits[0], (SEQS, LEN, D), 1.0, 6.0, ((1, 8),)),
        "pre_scales": jnp.clip(1.0 + 0.1 * jax.random.normal(splits[1], (D,), jnp.float32), 0.5, 1.5),
        "query_weight": noise(splits[2], (D, HEADS * DK), D ** -0.5, 0.125, ((1, 4),)),
        "key_weight": noise(splits[3], (D, HEADS * DK), D ** -0.5, 0.125, ((1, 4),)),
        "value_weight": noise(splits[4], (D, HEADS * DV), D ** -0.5, 0.125, ((1, 4),)),
        "swish_weight": noise(splits[5], (D, HEADS * DV), D ** -0.5, 0.125, ((1, 4),)),
        "projection": noise(splits[6], (HEADS * DV, D), (HEADS * DV) ** -0.5, 0.109375, ((0, 4),)),
        "mid_scales": jnp.clip(1.0 + 0.1 * jax.random.normal(splits[7], (D,), jnp.float32), 0.5, 1.5),
        "gelu_weight": noise(splits[8], (D, FF), D ** -0.5, 0.125, ((1, 4),)),
        "linear_weight": noise(splits[9], (D, FF), D ** -0.5, 0.125, ((1, 4),)),
        "down_weight": noise(splits[10], (FF, D), FF ** -0.5, 0.109375, ((0, 4),)),
        "cotangent": bell_draw_with(splits[11], (SEQS, LEN, D), 1.0, 6.0, ((1, 8),), (1, 2, 8, 2.0)),
    }


def layer_norm(values, scales):
    center = values - lax.optimization_barrier(jnp.mean(values, axis=-1, keepdims=True))
    spread = lax.optimization_barrier(jnp.mean(center * center, axis=-1, keepdims=True))
    return center * lax.rsqrt(spread + 1e-05) * scales

def group_norm(values):
    center = values - lax.optimization_barrier(jnp.mean(values, axis=-1, keepdims=True))
    spread = lax.optimization_barrier(jnp.mean(center * center, axis=-1, keepdims=True))
    return center * lax.rsqrt(spread + 1e-05)

def rotate(values, cosine_table, sine_table):
    half_dim = values.shape[-1] // 2
    leading = values[..., :half_dim]
    trailing = values[..., half_dim:]
    return jnp.concatenate([leading * cosine_table - trailing * sine_table, trailing * cosine_table + leading * sine_table], axis=-1)

def unrotate(values, cosine_table, sine_table):
    half_dim = values.shape[-1] // 2
    leading = values[..., :half_dim]
    trailing = values[..., half_dim:]
    return jnp.concatenate([leading * cosine_table + trailing * sine_table, trailing * cosine_table - leading * sine_table], axis=-1)

def angle_tables(positions, key_dim):
    half_dim = key_dim // 2
    frequency = 10000.0 ** (-jnp.arange(half_dim, dtype=jnp.float32) / half_dim)
    angles = positions[:, None] * frequency[None, :]
    return (jnp.cos(angles)[:, None, :], jnp.sin(angles)[:, None, :])

def decay_tables(decays, block_len):
    offsets = jnp.arange(block_len, dtype=jnp.float32)
    after_decay = decays[None, :] ** (offsets[:, None] + 1.0)
    before = decays[None, :] ** (block_len - 1.0 - offsets[:, None])
    distance = offsets[:, None] - offsets[None, :]
    within = jnp.where(distance[None] >= 0, decays[:, None, None] ** jnp.maximum(distance, 0.0)[None], 0.0)
    block_decay = decays ** float(block_len)
    return (after_decay, before, within, block_decay)

def swish_gate(normed, preact):
    return normed * jax.nn.silu(preact)

def gelu_gate(gating, linear):
    return jax.nn.gelu(gating) * linear

def matmul(left, right):
    return jnp.dot(left, right, preferred_element_type=jnp.float32)

def reference(block_input, pre_scales, query_weight, key_weight, value_weight, swish_weight, projection, mid_scales, gelu_weight, linear_weight, down_weight, cotangent):
    decays = 1.0 - 2.0 ** (-5.0 - jnp.arange(HEADS, dtype=jnp.float32))
    positions = jnp.arange(LEN, dtype=jnp.float32)
    cosine_table, sine_table = angle_tables(positions, DK)
    after_decay, before, within, block_decay = decay_tables(decays, BLK)
    blocks = LEN // BLK
    wide = jnp.float32

    def one_sequence(totals, paired):
        seq_input, seq_cotangent = paired
        input_float = seq_input.astype(wide)
        normed_input = layer_norm(input_float, pre_scales).astype(jnp.bfloat16)
        queries = matmul(normed_input, query_weight).reshape(LEN, HEADS, DK)
        key_pre = matmul(normed_input, key_weight).reshape(LEN, HEADS, DK)
        values = matmul(normed_input, value_weight).astype(jnp.bfloat16).reshape(blocks, BLK, HEADS, DV)
        swish_pre = matmul(normed_input, swish_weight)
        rotated_query = rotate(queries, cosine_table, sine_table).astype(jnp.bfloat16).reshape(blocks, BLK, HEADS, DK)
        rotated_key = rotate(key_pre, cosine_table, sine_table).astype(jnp.bfloat16).reshape(blocks, BLK, HEADS, DK)
        query_wide = rotated_query.astype(wide)
        key_wide = rotated_key.astype(wide)
        value_wide = values.astype(wide)
        scores = jnp.einsum('bthk,bmhk->bhtm', query_wide, key_wide)
        weights = (scores * within[None]).astype(jnp.bfloat16)
        inside = jnp.einsum('bhtm,bmhv->bthv', weights.astype(wide), value_wide)
        decayed = (value_wide * before[None, :, :, None]).astype(jnp.bfloat16)
        local_state = jnp.einsum('bthk,bthv->bhkv', key_wide, decayed.astype(wide))

        def chain_step(running, addend):
            return (block_decay[:, None, None] * running + addend, running)
        start_state = jnp.zeros((HEADS, DK, DV), wide)
        _, carried = lax.scan(chain_step, start_state, local_state)
        carried_bf16 = carried.astype(jnp.bfloat16)
        retained = inside + after_decay[None, :, :, None] * jnp.einsum('bthk,bhkv->bthv', query_wide, carried_bf16.astype(wide))
        normed_ret = group_norm(retained).reshape(LEN, HEADS * DV)
        gated_out = swish_gate(normed_ret, swish_pre).astype(jnp.bfloat16)
        residual = input_float + matmul(gated_out, projection)
        normed_mid = layer_norm(residual, mid_scales).astype(jnp.bfloat16)
        gate_pre = matmul(normed_mid, gelu_weight)
        linear_pre = matmul(normed_mid, linear_weight)
        hidden = gelu_gate(gate_pre, linear_pre).astype(jnp.bfloat16)
        output_sum = (residual + matmul(hidden, down_weight)).astype(jnp.bfloat16)
        hidden_back = matmul(seq_cotangent, down_weight.T)
        _, gelu_pull = jax.vjp(gelu_gate, gate_pre, linear_pre)
        gate_back, linear_back = gelu_pull(hidden_back)
        gate_back = gate_back.astype(jnp.bfloat16)
        linear_back = linear_back.astype(jnp.bfloat16)
        down_term = matmul(hidden.T, seq_cotangent)
        gelu_term = matmul(normed_mid.T, gate_back)
        linear_term = matmul(normed_mid.T, linear_back)
        mid_back = matmul(gate_back, gelu_weight.T) + matmul(linear_back, linear_weight.T)
        _, mid_pull = jax.vjp(layer_norm, residual, mid_scales)
        residual_back, mid_term = mid_pull(mid_back)
        residual_grad = seq_cotangent.astype(wide) + residual_back
        residual_bf16 = residual_grad.astype(jnp.bfloat16)
        projection_term = matmul(gated_out.T, residual_bf16)
        gated_back = matmul(residual_bf16, projection.T)
        _, swish_pull = jax.vjp(swish_gate, normed_ret, swish_pre)
        normed_back, swish_back = swish_pull(gated_back)
        _, group_pull = jax.vjp(group_norm, retained)
        retained_back = group_pull(normed_back.reshape(retained.shape))[0]
        retained_bf16 = retained_back.astype(jnp.bfloat16)
        back_wide = retained_bf16.astype(wide)
        score_back = (jnp.einsum('bthv,bmhv->bhtm', back_wide, value_wide) * within[None]).astype(jnp.bfloat16)
        weighted_back = (retained_back * after_decay[None, :, :, None]).astype(jnp.bfloat16)
        state_term = jnp.einsum('bthk,bthv->bhkv', query_wide, weighted_back.astype(wide))
        _, later_sum = lax.scan(chain_step, start_state, state_term, reverse=True)
        later_bf16 = later_sum.astype(jnp.bfloat16).astype(wide)
        score_wide = score_back.astype(wide)
        rotated_qgrad = jnp.einsum('bhtm,bmhk->bthk', score_wide, key_wide) + after_decay[None, :, :, None] * jnp.einsum('bthv,bhkv->bthk', back_wide, carried_bf16.astype(wide))
        rotated_kgrad = jnp.einsum('bhtm,bthk->bmhk', score_wide, query_wide) + jnp.einsum('bthv,bhkv->bthk', decayed.astype(wide), later_bf16)
        value_back = jnp.einsum('bhtm,bthv->bmhv', weights.astype(wide), back_wide) + before[None, :, :, None] * jnp.einsum('bthk,bhkv->bthv', key_wide, later_bf16)
        query_back = unrotate(rotated_qgrad.reshape(LEN, HEADS, DK), cosine_table, sine_table).astype(jnp.bfloat16).reshape(LEN, HEADS * DK)
        key_back = unrotate(rotated_kgrad.reshape(LEN, HEADS, DK), cosine_table, sine_table).astype(jnp.bfloat16).reshape(LEN, HEADS * DK)
        value_bf16 = value_back.astype(jnp.bfloat16).reshape(LEN, HEADS * DV)
        swish_bf16 = swish_back.astype(jnp.bfloat16)
        query_term = matmul(normed_input.T, query_back)
        key_term = matmul(normed_input.T, key_back)
        value_term = matmul(normed_input.T, value_bf16)
        swish_term = matmul(normed_input.T, swish_bf16)
        input_back = matmul(query_back, query_weight.T) + matmul(key_back, key_weight.T) + matmul(value_bf16, value_weight.T) + matmul(swish_bf16, swish_weight.T)
        _, input_pull = jax.vjp(layer_norm, input_float, pre_scales)
        input_return, pre_term = input_pull(input_back)
        input_grad = residual_grad + input_return
        terms = (pre_term, query_term, key_term, value_term, swish_term, projection_term, mid_term, gelu_term, linear_term, down_term)
        new_totals = tuple((left + right for left, right in zip(totals, terms)))
        return (new_totals, (output_sum, input_grad))
    start = (jnp.zeros((D,), wide), jnp.zeros(query_weight.shape, wide), jnp.zeros(key_weight.shape, wide), jnp.zeros(value_weight.shape, wide), jnp.zeros(swish_weight.shape, wide), jnp.zeros(projection.shape, wide), jnp.zeros((D,), wide), jnp.zeros(gelu_weight.shape, wide), jnp.zeros(linear_weight.shape, wide), jnp.zeros(down_weight.shape, wide))
    totals, stacked = lax.scan(one_sequence, start, (block_input, cotangent))
    return (stacked[0], stacked[1], totals[0], totals[1], totals[2], totals[3], totals[4], totals[5], totals[6], totals[7], totals[8], totals[9])
```

```python
import jax
import jax.numpy as jnp
from jax import lax
from jax.experimental import pallas as pl
from jax.experimental.pallas import tpu as pltpu
from jax.sharding import PartitionSpec as P

DK = 256
DV = 432
BF = jnp.bfloat16
WIDE = jnp.float32
BOTH = ("seq", "head")


def layer_norm(values, scales):
    center = values - jnp.mean(values, axis=-1, keepdims=True)
    spread = jnp.mean(center * center, axis=-1, keepdims=True)
    return center * lax.rsqrt(spread + 1e-05) * scales


def group_norm(values):
    center = values - jnp.mean(values, axis=-1, keepdims=True)
    spread = jnp.mean(center * center, axis=-1, keepdims=True)
    return center * lax.rsqrt(spread + 1e-05)


def rotate(values, cosine_table, sine_table):
    half_dim = values.shape[-1] // 2
    leading = values[..., :half_dim]
    trailing = values[..., half_dim:]
    return jnp.concatenate(
        [
            leading * cosine_table - trailing * sine_table,
            trailing * cosine_table + leading * sine_table,
        ],
        axis=-1,
    )


def swish_gate(normed, preact):
    return normed * jax.nn.silu(preact)


def gelu_gate(gating, linear):
    return jax.nn.gelu(gating) * linear


def matmul(left, right):
    return jnp.dot(left, right, preferred_element_type=WIDE)


def ein(spec, left, right):
    return jnp.einsum(spec, left, right, preferred_element_type=WIDE)


class Grid:
    def __init__(self, mesh_shape, tokens_here, width):
        self.n, self.h = mesh_shape["seq"], mesh_shape["head"]
        group = self.n
        while group % 4 == 0 and group * tokens_here > width:
            group //= 2
        self.group = group
        self.groups = self.n // group
        self.y = 2
        self.z = group // self.y
        self.c = 2
        self.x = self.h // self.c

    def digits(self, seq, head):
        return (seq // self.group, seq % self.group // self.y, seq % self.y, head // self.c, head % self.c)

    def flat(self, g, z, y, x, c):
        return ((g * self.z + z) * self.y + y) * self.h + x * self.c + c

    def send(self, value, step):
        pairs = []
        for seq in range(self.n):
            for head in range(self.h):
                g, z, y, x, c = self.digits(seq, head)
                dz, dy, dx, dc = step(c)
                there = self.flat(g, (z + dz) % self.z, (y + dy) % self.y, (x + dx) % self.x, (c + dc) % self.c)
                pairs.append((seq * self.h + head, there))
        return lax.ppermute(value, BOTH, pairs)


def assemble_body(core_ref, v, b, d, e, ov, ob, od, oe, out):
    rows = v.shape[1]

    def write(block, parts):
        for j, part in enumerate(parts):
            out[block, :, j * rows : (j + 1) * rows, :] = part[...].astype(BF)

    @pl.when(core_ref[0] == 0)
    def _():
        write(0, (v, b, ov, od))
        write(1, (d, e, ob, oe))

    @pl.when(core_ref[0] != 0)
    def _():
        write(0, (v, d, ov, ob))
        write(1, (b, e, od, oe))


def assemble(core, pieces):
    seqs, rows, width = pieces[0].shape
    cols = 512
    return pl.pallas_call(
        assemble_body,
        grid_spec=pltpu.PrefetchScalarGridSpec(
            num_scalar_prefetch=1,
            grid=(width // cols,),
            in_specs=[pl.BlockSpec((seqs, rows, cols), lambda i, core: (0, 0, i))] * len(pieces),
            out_specs=pl.BlockSpec((2, seqs, rows * 4, cols), lambda i, core: (0, 0, 0, i)),
        ),
        out_shape=jax.ShapeDtypeStruct((2, seqs, rows * 4, width), BF),
        name="assemble",
    )(core, *pieces)


def gather_group(grid, core, piece):
    chunks = []
    for k in range(grid.z):
        v = piece if k == 0 else grid.send(piece, lambda c: (k, 0, 0, 0))
        b = grid.send(v, lambda c: (0, c % 2, 1 - c % 2, 0))
        d = grid.send(v, lambda c: (0, 1 - c % 2, c % 2, 0))
        e = grid.send(b, lambda c: (0, 1 - c % 2, c % 2, 0))
        other = [grid.send(part, lambda c: (0, 0, 0, 1)) for part in (v, b, d, e)]
        chunks.append(assemble(core, [v, b, d, e, *other]))
    return chunks


def scatter_head(grid, partial):
    seqs, rows, width = partial.shape
    half = rows // 2
    kept = partial[:, :half] + grid.send(partial[:, half:], lambda c: (0, 0, 0, 1))
    quarter = half // 2
    return kept[:, :quarter] + grid.send(kept[:, quarter:], lambda c: (0, 0, 1, 0))


def gather_head(grid, piece):
    across = grid.send(piece, lambda c: (0, 0, 1, 0))
    pair = jnp.concatenate([piece, across], axis=1)
    return jnp.concatenate([pair, grid.send(pair, lambda c: (0, 0, 0, 1))], axis=1)


def on_device(
    grid,
    block_input,
    pre_scales,
    query_weight,
    key_weight,
    value_weight,
    swish_weight,
    projection,
    mid_scales,
    gelu_weight,
    linear_weight,
    down_weight,
    cotangent,
):
    seqs, block_len, width = block_input.shape
    rows = block_len // grid.h
    heads_here = query_weight.shape[1] // DK
    seq_at, head_at = lax.axis_index("seq"), lax.axis_index("head")
    core = (head_at % grid.c).astype(jnp.int32).reshape(1)

    x_at, c_at = head_at // grid.c, head_at % grid.c
    quarters = jnp.stack([((x_at + jx) % grid.x) * grid.c + (c_at + jc) % grid.c for jc in range(grid.c) for jx in range(grid.x)])
    offsets = (quarters[:, None] * rows + jnp.arange(rows)[None, :]).reshape(block_len).astype(WIDE)
    group_at, z_at, y_at = seq_at // grid.group, seq_at % grid.group // grid.y, seq_at % grid.y
    blocks = jnp.stack(
        [((z_at - k) % grid.z) * grid.y + (y_at + w) % grid.y for k in range(grid.z) for w in range(grid.y)]
    )

    head_start = (head_at * heads_here).astype(WIDE)
    decays = 1.0 - 2.0 ** (-5.0 - (head_start + jnp.arange(heads_here, dtype=WIDE)))
    after = decays[None, :] ** (offsets[:, None] + 1.0)
    before = decays[None, :] ** (block_len - 1.0 - offsets[:, None])
    distance = offsets[:, None] - offsets[None, :]
    within = jnp.where(distance[None] >= 0, decays[:, None, None] ** jnp.maximum(distance, 0.0)[None], 0.0)
    after_w = after[None, None, :, :, None]
    before_w = before[None, None, :, :, None]
    half_dim = DK // 2
    frequency = 10000.0 ** (-jnp.arange(half_dim, dtype=WIDE) / half_dim)
    starts = (group_at * grid.group + blocks).astype(WIDE) * block_len
    angles = (starts[:, None] + offsets[None, :])[:, :, None] * frequency
    cosine = jnp.cos(angles)[:, None, :, None, :]
    sine = jnp.sin(angles)[:, None, :, None, :]
    apart = (blocks[:, None] - blocks[None, :]).astype(WIDE)
    steps = block_len * (jnp.abs(apart) - 1.0)
    reach = decays[:, None, None] ** jnp.maximum(steps, 0.0)[None]
    earlier = jnp.where(apart[None] > 0, reach, 0.0)
    later = jnp.where(apart[None] < 0, reach, 0.0)

    def quarter(whole):
        return lax.dynamic_slice_in_dim(whole, head_at * rows, rows, 1).astype(WIDE)

    def in_place(relative):
        absolute = jnp.zeros_like(relative)
        for j in range(grid.h):
            part = relative[:, j * rows : (j + 1) * rows]
            absolute = lax.dynamic_update_slice_in_dim(absolute, part, quarters[j] * rows, 1)
        return absolute

    def slice_rows(parts):
        tall = jnp.concatenate([part.reshape(-1, width) for part in parts])
        mine = width // grid.n
        spread = tall.reshape(-1, grid.groups, grid.group, mine)
        return lax.dynamic_index_in_dim(spread, seq_at % grid.group, 2, keepdims=False).reshape(-1, grid.groups * mine)

    def total(term, axis):
        if grid.groups == 1:
            return term
        sets = [[g * grid.group + j for g in range(grid.groups)] for j in range(grid.group)]
        return lax.psum_scatter(term, "seq", scatter_dimension=axis, axis_index_groups=sets, tiled=True)

    def states_outside(sums, backwards):
        sets = [[g * grid.group + j for g in range(grid.groups)] for j in range(grid.group)]
        every = lax.all_gather(sums, "seq", axis_index_groups=sets)
        g = jnp.arange(grid.groups)
        gap = (g - group_at if backwards else group_at - g).astype(WIDE)
        weight = decays[:, None] ** (jnp.maximum(gap - 1.0, 0.0) * block_len * grid.group)[None, :]
        weight = jnp.where(gap[None] > 0, weight, 0.0)
        return jnp.sum(every * weight.T[:, None, :, None, None], axis=0)

    def carry(states, mix, backwards):
        inside_group = sum(mix.transpose(1, 2, 0)[:, c, None, :, None, None] * states[c][None] for c in range(grid.group))
        if grid.groups > 1:
            edge = (blocks if backwards else grid.group - 1 - blocks).astype(WIDE) * block_len
            sums = jnp.sum(states * (decays[None, :] ** edge[:, None])[:, None, :, None, None], axis=0)
            outside = states_outside(sums, backwards)
            reach_in = (grid.group - 1 - blocks if backwards else blocks).astype(WIDE) * block_len
            inside_group += (decays[None, :] ** reach_in[:, None])[:, None, :, None, None] * outside[None]
        return inside_group.astype(BF)

    input_q = quarter(block_input)
    normed_parts = gather_group(grid, core, layer_norm(input_q, pre_scales))
    cot_q = quarter(cotangent)
    cot_parts = gather_group(grid, core, cot_q)

    def split(parts, each):
        return jnp.concatenate(parts).reshape(grid.group, seqs, block_len, heads_here, each)

    def project(parts, weight):
        return [matmul(part.reshape(-1, width), weight) for part in parts]

    queries = split(project(normed_parts, query_weight), DK)
    keys = split(project(normed_parts, key_weight), DK)
    values = split([part.astype(BF) for part in project(normed_parts, value_weight)], DV)
    swish_pre = jnp.concatenate(project(normed_parts, swish_weight))
    rotated_query = rotate(queries, cosine, sine).astype(BF)
    rotated_key = rotate(keys, cosine, sine).astype(BF)
    scores = ein("bsthk,bsmhk->bshtm", rotated_query, rotated_key)
    weights = (scores * within[None, None]).astype(BF)
    inside = ein("bshtm,bsmhv->bsthv", weights, values)
    decayed = (values.astype(WIDE) * before_w).astype(BF)
    local = ein("bsthk,bsthv->bshkv", rotated_key, decayed)
    carried = carry(local, earlier, False)
    retained = inside + after_w * ein("bsthk,bshkv->bsthv", rotated_query, carried)
    normed_ret = group_norm(retained).reshape(-1, heads_here * DV)
    gated_out = swish_gate(normed_ret, swish_pre).astype(BF)

    own = seqs * block_len
    mixer = matmul(gated_out[:own], projection).reshape(seqs, block_len, width)
    residual_q = input_q + scatter_head(grid, mixer)
    mid_parts = gather_group(grid, core, layer_norm(residual_q, mid_scales))

    def feed(mid, cot):
        gate_pre = matmul(mid, gelu_weight)
        linear_pre = matmul(mid, linear_weight)
        hidden = gelu_gate(gate_pre, linear_pre).astype(BF)
        hidden_back = matmul(cot, down_weight.T)
        _, gelu_pull = jax.vjp(gelu_gate, gate_pre, linear_pre)
        gate_back, linear_back = gelu_pull(hidden_back)
        return hidden, gate_back.astype(BF), linear_back.astype(BF)

    def rows_of(parts):
        first = parts[0].reshape(-1, width)
        return [first[:own], first[own:]] + [part.reshape(-1, width) for part in parts[1:]]

    fed = [feed(mid, cot) for mid, cot in zip(rows_of(mid_parts), rows_of(cot_parts))]
    hidden_own, gate_own, linear_own = fed[0]
    mid_part = matmul(gate_own, gelu_weight.T) + matmul(linear_own, linear_weight.T)
    mid_back = scatter_head(grid, mid_part.reshape(seqs, block_len, width))
    _, mid_pull = jax.vjp(layer_norm, residual_q, mid_scales)
    residual_back, mid_term = mid_pull(mid_back)
    residual_grad = cot_q + residual_back
    back_parts = gather_group(grid, core, residual_grad)

    summed = scatter_head(grid, matmul(hidden_own, down_weight).reshape(seqs, block_len, width))
    block_output = in_place(gather_head(grid, residual_q + summed)).astype(BF)

    hidden, gate_back, linear_back = (jnp.concatenate([piece[i] for piece in fed]) for i in range(3))
    mid_slice = slice_rows(mid_parts)
    down_grad = total(matmul(hidden.T, slice_rows(cot_parts)), 1)
    gelu_grad = total(matmul(mid_slice.T, gate_back), 0)
    linear_grad = total(matmul(mid_slice.T, linear_back), 0)

    gated_back = jnp.concatenate(project(back_parts, projection.T))
    projection_grad = total(matmul(gated_out.T, slice_rows(back_parts)), 1)
    _, swish_pull = jax.vjp(swish_gate, normed_ret, swish_pre)
    normed_back, swish_back = swish_pull(gated_back)
    _, group_pull = jax.vjp(group_norm, retained)
    retained_back = group_pull(normed_back.reshape(retained.shape))[0]
    retained_bf16 = retained_back.astype(BF)
    score_back = (ein("bsthv,bsmhv->bshtm", retained_bf16, values) * within[None, None]).astype(BF)
    weighted_back = (retained_back * after_w).astype(BF)
    state_term = ein("bsthk,bsthv->bshkv", rotated_query, weighted_back)
    later_bf16 = carry(state_term, later, True)
    rotated_qgrad = ein("bshtm,bsmhk->bsthk", score_back, rotated_key) + after_w * ein(
        "bsthv,bshkv->bsthk", retained_bf16, carried
    )
    rotated_kgrad = ein("bshtm,bsthk->bsmhk", score_back, rotated_query) + ein(
        "bsthv,bshkv->bsthk", decayed, later_bf16
    )
    value_back = ein("bshtm,bsthv->bsmhv", weights, retained_bf16) + before_w * ein(
        "bsthk,bshkv->bsthv", rotated_key, later_bf16
    )
    query_back = rotate(rotated_qgrad, cosine, -sine).astype(BF).reshape(-1, heads_here * DK)
    key_back = rotate(rotated_kgrad, cosine, -sine).astype(BF).reshape(-1, heads_here * DK)
    value_bf16 = value_back.astype(BF).reshape(-1, heads_here * DV)
    swish_bf16 = swish_back.astype(BF)
    input_part = (
        matmul(query_back[:own], query_weight.T)
        + matmul(key_back[:own], key_weight.T)
        + matmul(value_bf16[:own], value_weight.T)
        + matmul(swish_bf16[:own], swish_weight.T)
    )
    input_back = scatter_head(grid, input_part.reshape(seqs, block_len, width))
    _, input_pull = jax.vjp(layer_norm, input_q, pre_scales)
    input_return, pre_term = input_pull(input_back)
    input_grad = in_place(gather_head(grid, residual_grad + input_return))

    normed_slice = slice_rows(normed_parts)
    query_grad = total(matmul(normed_slice.T, query_back), 0)
    key_grad = total(matmul(normed_slice.T, key_back), 0)
    value_grad = total(matmul(normed_slice.T, value_bf16), 0)
    swish_grad = total(matmul(normed_slice.T, swish_bf16), 0)
    gains = lax.psum(jnp.stack([pre_term, mid_term]), BOTH)
    gain_len = width // grid.n
    gains = lax.dynamic_slice_in_dim(gains, seq_at * gain_len, gain_len, 1)
    return (
        block_output,
        input_grad,
        gains[0],
        query_grad,
        key_grad,
        value_grad,
        swish_grad,
        projection_grad,
        gains[1],
        gelu_grad,
        linear_grad,
        down_grad,
    )


def solution(mesh):
    in_specs = (
        P(None, "seq", None),
        P(),
        P(None, "head"),
        P(None, "head"),
        P(None, "head"),
        P(None, "head"),
        P("head", None),
        P(),
        P(None, "head"),
        P(None, "head"),
        P("head", None),
        P(None, "seq", None),
    )
    out_specs = (
        P(None, "seq", None),
        P(None, "seq", None),
        P("seq"),
        P("seq", "head"),
        P("seq", "head"),
        P("seq", "head"),
        P("seq", "head"),
        P("head", "seq"),
        P("seq"),
        P("seq", "head"),
        P("seq", "head"),
        P("head", "seq"),
    )

    def run(*arrays):
        tokens_here = arrays[0].shape[0] * arrays[0].shape[1] // mesh.shape["seq"]
        grid = Grid(mesh.shape, tokens_here, arrays[0].shape[2])
        return jax.shard_map(
            lambda *shards: on_device(grid, *shards),
            mesh=mesh,
            in_specs=in_specs,
            out_specs=out_specs,
            check_vma=False,
        )(*arrays)

    return run
```

```python
import jax
import jax.numpy as jnp
from jax import lax
from jax.experimental import pallas as pl
from jax.experimental.pallas import tpu as pltpu
from jax.sharding import Mesh
from jax.sharding import PartitionSpec as P


DK = 256
DV = 432
BF = jnp.bfloat16
WIDE = jnp.float32
ALL = ("seq", "x", "core")
NT = (((1,), (1,)), ((), ()))
TN = (((0,), (0,)), ((), ()))
NN = (((1,), (0,)), ((), ()))
VMEM_BYTES = 58 * 1024 * 1024


def layer_norm(values, scales):
    center = values - jnp.mean(values, axis=-1, keepdims=True)
    spread = jnp.mean(center * center, axis=-1, keepdims=True)
    return center * lax.rsqrt(spread + 1e-05) * scales


def gelu_gate(gating, linear):
    return jax.nn.gelu(gating) * linear


def matmul(left, right):
    return jnp.dot(left, right, preferred_element_type=WIDE)


def dot(left, right, dims):
    return lax.dot_general(left, right, dims, preferred_element_type=WIDE)


class Grid:
    def __init__(self, mesh_shape, tokens_here, width):
        self.n, self.h = mesh_shape["seq"], mesh_shape["head"]
        group = self.n
        while group % 4 == 0 and group * tokens_here > width:
            group //= 2
        self.group = group
        self.groups = self.n // group
        self.y = 2
        self.z = group // self.y
        self.c = 2
        self.x = self.h // self.c

    def send(self, value, dz=0, dy=0, dx=0, dc=0, dg=0, swap=False):
        pairs = []
        for seq in range(self.n):
            for head in range(self.h):
                g, z, y = seq // self.group, seq % self.group // self.y, seq % self.y
                x, c = head // self.c, head % self.c
                ey, ex = (dx, dy) if swap and c else (dy, dx)
                g, z, y = (g + dg) % self.groups, (z + dz) % self.z, (y + ey) % self.y
                x, c = (x + ex) % self.x, (c + dc) % self.c
                pairs.append((seq * self.h + head, ((g * self.z + z) * self.y + y) * self.h + x * self.c + c))
        return lax.ppermute(value, ALL, pairs)

    def sum_all(self, value):
        for digit, size in (("dc", self.c), ("dx", self.x), ("dy", self.y), ("dz", self.z), ("dg", self.groups)):
            step = 1
            while step < size:
                value = value + self.send(value, **{digit: step})
                step *= 2
        return value


def gather_pieces(grid, piece, k):
    v = piece if k == 0 else grid.send(piece, dz=k)
    b = grid.send(v, dx=1, swap=True)
    d = grid.send(v, dy=1, swap=True)
    e = grid.send(b, dy=1, swap=True)
    other = [grid.send(part, dc=1) for part in (v, b, d, e)]
    return [v, b, d, e, *other]


def gather_along_seq(grid, piece):
    found = []
    for k in range(grid.z):
        v = piece if k == 0 else grid.send(piece, dz=k)
        pair = [v, grid.send(v, dy=1)]
        found.append(pair + [grid.send(part, dc=1) for part in pair])
    return found


def scatter_head(grid, keep, give):
    here = keep + grid.send(give, dc=1)
    return here[0] + grid.send(here[1], dx=1)


def picks(c):
    return (0, 1 + c, 4, 6 - c), (2 - c, 3, 5 + c, 7)


def start_all(sources, targets, sem, first=0):
    copies = [pltpu.make_async_copy(a, b, sem.at[first + i]) for i, (a, b) in enumerate(zip(sources, targets))]
    for copy in copies:
        copy.start()
    return copies


def build(x, buf, c, first=0):
    _, seqs, rows, _ = buf.shape
    for block, indices in enumerate(picks(c)):
        for s in range(seqs):
            for j, at in enumerate(indices):
                row = ((block * seqs + s) * 4 + j) * rows
                x[row : row + rows, :] = buf[first + at, s].astype(BF)


def turn(values, cosine, sine):
    half = values.shape[-1] // 2
    a, b = values[:, :half], values[:, half:]
    return jnp.concatenate([a * cosine - b * sine, b * cosine + a * sine], axis=-1)


def standard(values):
    center = values - jnp.mean(values, axis=-1, keepdims=True)
    inverse = lax.rsqrt(jnp.mean(center * center, axis=-1, keepdims=True) + 1e-05)
    return center * inverse, inverse


def my_columns(x, col, mine):
    return x[:, pl.ds(pl.multiple_of(col * mine, mine), mine)]


def project_body(heads, seqs, core, col, *refs):
    pieces, (wq, wk, wv, ws) = refs[:8], refs[8:12]
    cosine, sine, before, weigh = refs[12:16]
    old_state = refs[-14]
    rq, rk, values, swish, mine, state = refs[-13:-7]
    buf, bq, bk, bv, bs, x, sem = refs[-7:]
    arrive = start_all(pieces, [buf.at[i] for i in range(8)], sem)
    weights = start_all((wq, wk, wv, ws), (bq, bk, bv, bs), sem, 8)
    for copy in arrive:
        copy.wait()
    build(x, buf, core[0])
    mine[...] = my_columns(x, col[0], mine.shape[1])
    rows = before.shape[1]
    blocks = x.shape[0] // (seqs * rows)

    def at(block, s):
        start = (block * seqs + s) * rows
        return slice(start, start + rows)

    for out, source, copy in ((rk, bk, weights[1]), (rq, bq, weights[0])):
        copy.wait()
        for h in range(heads):
            raw = dot(x[...], source[:, h * DK : (h + 1) * DK], NN)
            for block in range(blocks):
                for s in range(seqs):
                    out[h, at(block, s), :] = turn(raw[at(block, s)], cosine[block], sine[block]).astype(BF)
    weights[2].wait()
    for h in range(heads):
        values[h] = dot(x[...], bv[h * DV : (h + 1) * DV, :], NT).astype(BF)
    weights[3].wait()
    for h in range(heads):
        swish[h] = dot(x[...], bs[h * DV : (h + 1) * DV, :], NT)
    for h in range(heads):
        for s in range(seqs):
            kept = jnp.concatenate([rk[h, at(block, s), :] for block in range(blocks)])
            decayed = jnp.concatenate(
                [
                    (values[h, at(block, s), :].astype(WIDE) * (before[h] * weigh[h, block])).astype(BF)
                    for block in range(blocks)
                ]
            )
            state[h, s] = old_state[h, s] + dot(kept, decayed, TN)


def full(shape):
    return pl.BlockSpec(shape, lambda *_: (0,) * len(shape))


ANY = pl.BlockSpec(memory_space=pl.ANY)
SMEM = pl.BlockSpec(memory_space=pltpu.SMEM)


def chunk_block(shape, chunk):
    heads, rows, width = shape
    return pl.BlockSpec((heads, rows, width), lambda *_: (0, chunk, 0))


def chunk_call(body, scalars, args, arg_specs, outs, so_far, carried_over, scratch, chunk, chunks):
    filled = [] if so_far is None else list(so_far)
    out_shape, out_specs = [], []
    for shape, kind in outs:
        if len(shape) == 3:
            out_shape.append(jax.ShapeDtypeStruct((shape[0], shape[1] * chunks, shape[2]), kind))
            out_specs.append(chunk_block(shape, chunk))
        else:
            out_shape.append(jax.ShapeDtypeStruct((shape[0] * chunks, shape[1]), kind))
            out_specs.append(pl.BlockSpec(shape, lambda *_: (chunk, 0)))
    for a in carried_over:
        out_shape.append(jax.ShapeDtypeStruct(a.shape, a.dtype))
        out_specs.append(full(a.shape))
    aliases = {}
    at = len(scalars) + len(args)
    for i in range(len(filled)):
        aliases[at + i] = i
    for i in range(len(carried_over)):
        aliases[at + len(filled) + i] = len(outs) + i
    call = pl.pallas_call(
        body,
        grid_spec=pltpu.PrefetchScalarGridSpec(
            num_scalar_prefetch=len(scalars),
            grid=(1,),
            in_specs=[*arg_specs, *[ANY] * len(filled), *(full(a.shape) for a in carried_over)],
            out_specs=out_specs,
            scratch_shapes=scratch,
        ),
        out_shape=out_shape,
        input_output_aliases=aliases,
        compiler_params=pltpu.CompilerParams(vmem_limit_bytes=VMEM_BYTES),
    )
    result = call(*scalars, *args, *filled, *carried_over)
    return result[: len(outs)], result[len(outs) :]


def piece_buffer(piece, sets=1):
    return pltpu.VMEM((8 * sets, *piece.shape), WIDE)


def forward_body(heads, seqs, order, within, after, before, through, rq, rk, values, start, ret, carried, final, state):
    step = pl.program_id(0)
    rows = within.shape[1]

    @pl.when(step == 0)
    def _():
        state[...] = start[...]

    for h in range(heads):
        for s in range(seqs):
            at = slice(s * rows, (s + 1) * rows)
            q, k, v = rq[h, at, :], rk[h, at, :], values[h, at, :]
            w = (dot(q, k, NT) * within[h]).astype(BF)
            held = state[h, s].astype(BF)
            carried[0, h, s] = held
            ret[h, at, :] = dot(w, v, NN) + after[h] * dot(q, held, NN)
            decayed = (v.astype(WIDE) * before[h]).astype(BF)
            state[h, s] = through[h] * state[h, s] + dot(k, decayed, TN)

    @pl.when(step == pl.num_programs(0) - 1)
    def _():
        final[...] = state[...]


def by_block(array, tile):
    heads, _, width = array.shape
    return pl.BlockSpec((heads, tile, width), lambda i, order: (0, order[i], 0))


def retention_forward(order, tables, rq, rk, values, start):
    heads, seqs, dk, dv = start.shape
    within, after, before, through = tables
    blocks = order.shape[0]
    tile = rq.shape[1] // blocks
    states = pl.BlockSpec((1, heads, seqs, dk, dv), lambda i, order: (order[i], 0, 0, 0, 0))
    return pl.pallas_call(
        lambda *refs: forward_body(heads, seqs, *refs),
        grid_spec=pltpu.PrefetchScalarGridSpec(
            num_scalar_prefetch=1,
            grid=(blocks,),
            in_specs=[*(full(t.shape) for t in tables), *(by_block(a, tile) for a in (rq, rk, values)), full(start.shape)],
            out_specs=[by_block(values, tile), states, full(start.shape)],
            scratch_shapes=[pltpu.VMEM(start.shape, WIDE)],
        ),
        out_shape=[
            jax.ShapeDtypeStruct(values.shape, WIDE),
            jax.ShapeDtypeStruct((blocks, heads, seqs, dk, dv), BF),
            jax.ShapeDtypeStruct(start.shape, WIDE),
        ],
        compiler_params=pltpu.CompilerParams(vmem_limit_bytes=VMEM_BYTES),
        name="retention_forward",
    )(order, *tables, rq, rk, values, start)


def split_rows(keep, give, s, tall):
    shifts, _, rows, _ = keep.shape
    for jx in range(shifts):
        keep[jx, s] = tall[jx * rows : (jx + 1) * rows]
        give[jx, s] = tall[(shifts + jx) * rows : (shifts + jx + 1) * rows]


def own_forward_body(heads, seqs, within, after, rq, rk, values, swish, held, weight, keep, give, bw, sem):
    (copy,) = start_all((weight,), (bw,), sem)
    rows = within.shape[1]
    gated = []
    for s in range(seqs):
        at = slice(s * rows, (s + 1) * rows)
        for h in range(heads):
            q = rq[h, at, :]
            v = values[h, at, :]
            w = (dot(q, rk[h, at, :], NT) * within[h]).astype(BF)
            normed, _ = standard(dot(w, v, NN) + after[h] * dot(q, held[h, s].astype(BF), NN))
            p = swish[h, at, :]
            gated.append((normed * (p * jax.nn.sigmoid(p))).astype(BF))
    copy.wait()
    for s in range(seqs):
        split_rows(
            keep, give, s, sum(dot(gated[s * heads + h], bw[h * DV : (h + 1) * DV, :], NN) for h in range(heads))
        )


def own_call(body, tile, tables, arrays, states, weights, out_rows):
    heads, seqs = states[0].shape[:2]
    out = jax.ShapeDtypeStruct(out_rows, WIDE)
    return pl.pallas_call(
        lambda *refs: body(heads, seqs, *refs),
        grid=(1,),
        in_specs=[
            *(full(t.shape) for t in tables),
            *(pl.BlockSpec((heads, tile, a.shape[2]), lambda *_: (0, 0, 0)) for a in arrays),
            *(full(a.shape) for a in states),
            *[ANY] * len(weights),
        ],
        out_specs=[full(out_rows)] * 2,
        out_shape=[out, out],
        scratch_shapes=[*(pltpu.VMEM(w.shape, w.dtype) for w in weights), pltpu.SemaphoreType.DMA((len(weights),))],
        compiler_params=pltpu.CompilerParams(vmem_limit_bytes=VMEM_BYTES),
    )(*tables, *arrays, *states, *weights)


def own_rows_body(v, x, c, xc, out):
    seqs, rows, _ = v.shape
    for j, part in enumerate((v, x, c, xc)):
        for s in range(seqs):
            at = (j * seqs + s) * rows
            out[at : at + rows, :] = part[s].astype(BF)


def own_rows(pieces):
    seqs, rows, width = pieces[0].shape
    return pl.pallas_call(
        own_rows_body,
        grid=(1,),
        in_specs=[full(p.shape) for p in pieces],
        out_specs=full((4 * seqs * rows, width)),
        out_shape=jax.ShapeDtypeStruct((4 * seqs * rows, width), BF),
        name="own_rows",
    )(*pieces)


def feed_body(last, count, col, *refs):
    mids, cots, refs = refs[:count], refs[count : 2 * count], refs[2 * count :]
    weights, old, new = refs[:3], refs[3:6], refs[6:9]
    bufm, bufc, bg, bl, bd, sem = refs[9:]
    rows = bufm.shape[0] // count
    places = [pl.ds(i * rows, rows) for i in range(count)]
    arrive = start_all(mids, [bufm.at[at] for at in places], sem)
    arrive += start_all(cots, [bufc.at[at] for at in places], sem, count)
    copies = start_all(weights, (bg, bl, bd), sem, 2 * count)
    for copy in arrive:
        copy.wait()
    xm, xc = bufm[...].astype(BF), bufc[...].astype(BF)
    cols = old[0].shape[0]
    mid_t = my_columns(bufm, col[0], cols).T.astype(BF)
    cot_t = my_columns(bufc, col[0], cols).T.astype(BF)
    for copy in copies:
        copy.wait()
    hidden_units = bg.shape[0]
    half = hidden_units // 2
    root = 0.7978845608028654
    for i in range(2):
        at = slice(i * half, (i + 1) * half)
        a = dot(xm, bg[at, :], NT)
        linear = dot(xm, bl[at, :], NT)
        back = dot(xc, bd[at, :], NT)
        square = a * a
        t = jnp.tanh(root * (a * (1.0 + 0.044715 * square)))
        gelu = 0.5 * a * (1.0 + t)
        slope = 0.5 * (1.0 + t) + 0.5 * a * (1.0 - t * t) * (root * (1.0 + 3 * 0.044715 * square))
        hidden = (gelu * linear).astype(BF)
        gate_back = (back * linear * slope).astype(BF)
        linear_back = (back * gelu).astype(BF)
        for out, before, left, right in zip(new, old, (cot_t, mid_t, mid_t), (hidden, gate_back, linear_back)):
            term = before[:, at] + dot(left, right, NN)
            if last:
                out[at, :] = term.T
            else:
                out[:, at] = term


def feed(col, mids, cots, weights, sums, last):
    shape = sums[0].shape
    out_shape = shape[::-1] if last else shape
    count = len(cots)
    rows, width = cots[0].shape
    tokens = pltpu.VMEM((count * rows, width), WIDE)
    return pl.pallas_call(
        lambda *refs: feed_body(last, count, *refs),
        grid_spec=pltpu.PrefetchScalarGridSpec(
            num_scalar_prefetch=1,
            grid=(1,),
            in_specs=[*[ANY] * (2 * count + 3), *[full(shape)] * 3],
            out_specs=[full(out_shape)] * 3,
            scratch_shapes=[
                tokens,
                tokens,
                *(pltpu.VMEM(w.shape, w.dtype) for w in weights),
                pltpu.SemaphoreType.DMA((2 * count + 3,)),
            ],
        ),
        out_shape=[jax.ShapeDtypeStruct(out_shape, WIDE)] * 3,
        compiler_params=pltpu.CompilerParams(vmem_limit_bytes=VMEM_BYTES),
        name="feed",
    )(col, *mids, *cots, *weights, *sums)


def ungate_body(heads, seqs, core, col, *refs):
    pieces, weight = refs[:8], refs[8]
    ret, swish, rq, after, weigh = refs[9:14]
    old_state = refs[-12]
    sb, rb, wb, gated, mine, state = refs[-11:-5]
    buf, bw, x, back, sem = refs[-5:]
    arrive = start_all(pieces, [buf.at[i] for i in range(8)], sem)
    (copy,) = start_all((weight,), (bw,), sem, 8)
    for piece in arrive:
        piece.wait()
    build(x, buf, core[0])
    mine[...] = my_columns(x, col[0], mine.shape[1])
    rows = after.shape[1]
    blocks = x.shape[0] // (seqs * rows)
    copy.wait()
    for h in range(heads):
        back[...] = dot(x[...], bw[h * DV : (h + 1) * DV, :], NT)
        for s in range(seqs):
            kept, weighted = [], []
            for block in range(blocks):
                start = (block * seqs + s) * rows
                at = slice(start, start + rows)
                normed, inverse = standard(ret[h, at, :])
                p = swish[h, at, :]
                gate = jax.nn.sigmoid(p)
                silu = p * gate
                gated[h, at, :] = (normed * silu).astype(BF)
                g = back[at, :]
                sb[h, at, :] = (g * normed * (gate * (1.0 + p * (1.0 - gate)))).astype(BF)
                nb = g * silu
                r = inverse * (
                    nb - jnp.mean(nb, axis=-1, keepdims=True) - normed * jnp.mean(nb * normed, axis=-1, keepdims=True)
                )
                rb[h, at, :] = r.astype(BF)
                w = r * after[h]
                wb[h, at, :] = w.astype(BF)
                weighted.append((w * weigh[h, block]).astype(BF))
                kept.append(rq[h, at, :])
            state[h, s] = old_state[h, s] + dot(jnp.concatenate(kept), jnp.concatenate(weighted), TN)


def block_gradients(q, k, v, r, held, later, within, after, before, cosine, sine):
    w = (dot(q, k, NT) * within).astype(BF)
    score = (dot(r, v, NT) * within).astype(BF)
    decayed = (v.astype(WIDE) * before).astype(BF)
    qg = dot(score, k, NN) + after * dot(r, held, NT)
    kg = dot(score, q, TN) + dot(decayed, later, NT)
    vg = dot(w, r, TN) + before * dot(k, later, NN)
    return turn(qg, cosine, -sine).astype(BF), turn(kg, cosine, -sine).astype(BF), vg.astype(BF)


def own_backward_body(
    heads, seqs, cosine, sine, within, after, before, rq, rk, values, rb, sb, held, later, *refs
):
    weights, (keep, give), scratch = refs[:4], refs[4:6], refs[6:]
    copies = start_all(weights, scratch[:4], scratch[4])
    bq, bk, bv, bs = scratch[:4]
    rows = within.shape[1]
    found = []
    for s in range(seqs):
        at = slice(s * rows, (s + 1) * rows)
        found.append(
            [
                block_gradients(
                    rq[h, at, :],
                    rk[h, at, :],
                    values[h, at, :],
                    rb[h, at, :],
                    held[h, s].astype(BF),
                    later[h, s].astype(BF),
                    within[h],
                    after[h],
                    before[h],
                    cosine[0],
                    sine[0],
                )
                for h in range(heads)
            ]
        )
    for copy in copies:
        copy.wait()
    for s in range(seqs):
        at = slice(s * rows, (s + 1) * rows)
        tall = None
        for h in range(heads):
            qb, kb, vb = found[s][h]
            keys, cols = slice(h * DK, (h + 1) * DK), slice(h * DV, (h + 1) * DV)
            for term in (
                dot(qb, bq[:, keys], NT),
                dot(kb, bk[:, keys], NT),
                dot(vb, bv[cols, :], NN),
                dot(sb[h, at, :], bs[cols, :], NN),
            ):
                tall = term if tall is None else tall + term
        split_rows(keep, give, s, tall)


def backward_body(
    heads, seqs, order, cosine, sine, within, after, before, through, rq, rk, values, rb, wb, sb, gated, mine, mid,
    carried, start, gq, gk, gv, gs, gp, final, state, bq, bk, bv, aq, ak, av, asw, ap,
):
    step = pl.program_id(0)
    rows = within.shape[1]

    @pl.when(step == 0)
    def _():
        state[...] = start[...]
        for total in (aq, ak, av, asw, ap):
            total[...] = jnp.zeros_like(total)

    for h in range(heads):
        for s in range(seqs):
            at = slice(s * rows, (s + 1) * rows)
            q = rq[h, at, :]
            bq[h, at, :], bk[h, at, :], bv[h, at, :] = block_gradients(
                q,
                rk[h, at, :],
                values[h, at, :],
                rb[h, at, :],
                carried[0, h, s],
                state[h, s].astype(BF),
                within[h],
                after[h],
                before[h],
                cosine[0],
                sine[0],
            )
            state[h, s] = through[h] * state[h, s] + dot(q, wb[h, at, :], TN)
    left, right = mine[...].T, mid[...].T
    for h in range(heads):
        aq[h] += dot(left, bq[h], NN)
        ak[h] += dot(left, bk[h], NN)
        av[h] += dot(left, bv[h], NN)
        asw[h] += dot(left, sb[h], NN)
        ap[h] += dot(right, gated[h], NN)

    @pl.when(step == pl.num_programs(0) - 1)
    def _():
        final[...] = state[...]
        for h in range(heads):
            gq[:, h * DK : (h + 1) * DK] = aq[h]
            gk[:, h * DK : (h + 1) * DK] = ak[h]
            for out, total in ((gv, av), (gs, asw), (gp, ap)):
                out[h * DV : (h + 1) * DV, :] = total[h].T


def retention_backward(order, tables, token_args, slices, carried, start):
    heads, seqs, dk, dv = start.shape
    cosine, _ = tables[:2]
    blocks = order.shape[0]
    tile = token_args[0].shape[1] // blocks
    cols = slices[0].shape[1]
    angle = pl.BlockSpec((1, *cosine.shape[1:]), lambda i, order: (order[i], 0, 0))
    states = pl.BlockSpec((1, heads, seqs, dk, dv), lambda i, order: (order[i], 0, 0, 0, 0))
    outs = [(cols, heads * dk)] * 2 + [(heads * dv, cols)] * 3 + [start.shape]
    return pl.pallas_call(
        lambda *refs: backward_body(heads, seqs, *refs),
        grid_spec=pltpu.PrefetchScalarGridSpec(
            num_scalar_prefetch=1,
            grid=(blocks,),
            in_specs=[
                angle,
                angle,
                *(full(t.shape) for t in tables[2:]),
                *(by_block(a, tile) for a in token_args),
                *[pl.BlockSpec((tile, cols), lambda i, order: (order[i], 0))] * 2,
                states,
                full(start.shape),
            ],
            out_specs=[full(shape) for shape in outs],
            scratch_shapes=[
                pltpu.VMEM(start.shape, WIDE),
                *[pltpu.VMEM((heads, tile, dk), BF)] * 2,
                pltpu.VMEM((heads, tile, dv), BF),
                *[pltpu.VMEM((heads, cols, dk), WIDE)] * 2,
                *[pltpu.VMEM((heads, cols, dv), WIDE)] * 3,
            ],
        ),
        out_shape=[jax.ShapeDtypeStruct(shape, WIDE) for shape in outs],
        compiler_params=pltpu.CompilerParams(vmem_limit_bytes=VMEM_BYTES),
        name="retention_backward",
    )(order, *tables, *token_args, *slices, carried, start)


def place_body(places, *refs):
    parts, out = refs[:-1], refs[-1]
    rows = parts[0].shape[1]
    for j, part in enumerate(parts):
        out[:, pl.ds(pl.multiple_of(places[j] * rows, rows), rows), :] = part[...].astype(out.dtype)


def place(places, parts, kind):
    seqs, rows, width = parts[0].shape
    return pl.pallas_call(
        place_body,
        grid_spec=pltpu.PrefetchScalarGridSpec(
            num_scalar_prefetch=1,
            grid=(1,),
            in_specs=[full(part.shape) for part in parts],
            out_specs=full((seqs, rows * len(parts), width)),
        ),
        out_shape=jax.ShapeDtypeStruct((seqs, rows * len(parts), width), kind),
        name="place",
    )(places, *parts)


def gather_head(grid, piece):
    pair = [piece, grid.send(piece, dx=1)]
    return pair + [grid.send(part, dc=1) for part in pair]


def on_device(
    grid,
    block_input,
    pre_scales,
    query_weight,
    key_weight,
    value_weight,
    swish_weight,
    projection,
    mid_scales,
    gelu_weight,
    linear_weight,
    down_weight,
    cotangent,
):
    seqs, block_len, width = block_input.shape
    rows = block_len // grid.h
    heads = query_weight.shape[1] // DK
    hidden_units = gelu_weight.shape[1]
    tile = seqs * block_len
    chunk_rows = grid.y * tile
    seq_at, x_at, c_at = lax.axis_index("seq"), lax.axis_index("x"), lax.axis_index("core")
    head_at = x_at * grid.c + c_at
    group_at, z_at, y_at = seq_at // grid.group, seq_at % grid.group // grid.y, seq_at % grid.y
    peer = seq_at % grid.group
    core = c_at.astype(jnp.int32).reshape(1)
    col = peer.astype(jnp.int32).reshape(1)
    mine = width // grid.group

    j = jnp.arange(grid.h)
    quarters = ((x_at + j % grid.x) % grid.x) * grid.c + (c_at + j // grid.x) % grid.c
    places = quarters.astype(jnp.int32)
    offsets = (quarters[:, None] * rows + jnp.arange(rows)[None, :]).reshape(block_len).astype(WIDE)
    slot = jnp.arange(grid.group)
    blocks = ((z_at - slot // grid.y) % grid.z) * grid.y + (y_at + slot % grid.y) % grid.y
    order = (((z_at - slot // grid.y) % grid.z) * grid.y + (slot % grid.y - y_at) % grid.y).astype(jnp.int32)

    decays = 1.0 - 2.0 ** (-5.0 - ((head_at * heads).astype(WIDE) + jnp.arange(heads, dtype=WIDE)))
    after = (decays[:, None] ** (offsets[None, :] + 1.0))[:, :, None]
    before = (decays[:, None] ** (block_len - 1.0 - offsets[None, :]))[:, :, None]
    distance = offsets[:, None] - offsets[None, :]
    within = jnp.where(distance[None] >= 0, decays[:, None, None] ** jnp.maximum(distance, 0.0)[None], 0.0)
    through = jnp.broadcast_to((decays ** float(block_len))[:, None, None], (heads, 1, DV))
    half_dim = DK // 2
    frequency = 10000.0 ** (-jnp.arange(half_dim, dtype=WIDE) / half_dim)
    starts = (group_at * grid.group + blocks).astype(WIDE) * block_len
    angles = (starts[:, None] + offsets[None, :])[:, :, None] * frequency
    cosine, sine = jnp.cos(angles), jnp.sin(angles)
    gap = (peer - blocks).astype(WIDE)
    reach = decays[:, None] ** (block_len * jnp.maximum(jnp.abs(gap) - 1.0, 0.0))[None, :]
    weigh_earlier = jnp.where(gap[None] > 0, reach, 0.0)
    weigh_later = jnp.where(gap[None] < 0, reach, 0.0)
    no_state = jnp.zeros((heads, seqs, DK, DV), WIDE)

    def quarter(whole):
        return lax.dynamic_slice_in_dim(whole, head_at * rows, rows, 1).astype(WIDE)

    peers = [[g * grid.group + p for g in range(grid.groups)] for p in range(grid.group)]

    def total(term, axis):
        if grid.groups == 1:
            return term
        part = lax.psum_scatter(term, "seq", scatter_dimension=axis, axis_index_groups=peers, tiled=True)
        pairs = [(g * grid.group + p, p * grid.groups + g) for g in range(grid.groups) for p in range(grid.group)]
        return lax.ppermute(part, "seq", pairs)

    def outside(sums, backwards):
        every = lax.all_gather(sums, "seq", axis_index_groups=peers)
        g = jnp.arange(grid.groups)
        apart = (g - group_at if backwards else group_at - g).astype(WIDE)
        weight = decays[None, :] ** (jnp.maximum(apart - 1.0, 0.0) * block_len * grid.group)[:, None]
        weight = jnp.where(apart[:, None] > 0, weight, 0.0)
        found = jnp.sum(every * weight[:, :, None, None, None], axis=0)
        steps = (grid.group - 1 - peer if backwards else peer).astype(WIDE) * block_len
        return found, found * (decays**steps)[:, None, None, None]

    input_q = quarter(block_input)
    cot_q = quarter(cotangent)
    normed_q = layer_norm(input_q, pre_scales)
    arrays, state = None, [no_state]
    for k in chunk_order(grid.z):
        pieces = gather_pieces(grid, normed_q, k)
        near = slice(k * grid.y, (k + 1) * grid.y)
        piece = pieces[0]
        arrays, state = chunk_call(
            lambda *refs: project_body(heads, seqs, *refs),
            (core, col),
            [
                *pieces,
                query_weight,
                key_weight,
                value_weight.T,
                swish_weight.T,
                cosine[near],
                sine[near],
                before,
                weigh_earlier[:, near],
            ],
            [*[ANY] * 12, *[full((grid.y, *cosine.shape[1:]))] * 2, full(before.shape), SMEM],
            [
                ((heads, chunk_rows, DK), BF),
                ((heads, chunk_rows, DK), BF),
                ((heads, chunk_rows, DV), BF),
                ((heads, chunk_rows, DV), WIDE),
                ((chunk_rows, mine), BF),
            ],
            arrays,
            state,
            [
                piece_buffer(piece),
                *(pltpu.VMEM(w.shape, BF) for w in (query_weight, key_weight, value_weight.T, swish_weight.T)),
                pltpu.VMEM((chunk_rows, width), BF),
                pltpu.SemaphoreType.DMA((12,)),
            ],
            k,
            grid.z,
        )
    cot_pair = jnp.concatenate(
        [
            lax.dynamic_slice_in_dim(cotangent, ((x_at + x) % grid.x * grid.c + c_at) * rows, rows, 1).reshape(-1, width)
            for x in range(grid.x)
        ]
    ).astype(WIDE)
    cot_all = gather_along_seq(grid, cot_pair)
    rotated_query, rotated_key, values, swish_pre, normed_slice = arrays
    held = state[0]
    forward_tables = (within, after, before, through)
    edge = no_state
    if grid.groups > 1:
        _, _, sums = retention_forward(order, forward_tables, rotated_query, rotated_key, values, no_state)
        edge, here = outside(sums, False)
        held = held + here

    own_shape = (grid.x, seqs, rows, width)
    keep, give = own_call(
        own_forward_body,
        tile,
        (within, after),
        (rotated_query, rotated_key, values, swish_pre),
        (held,),
        (projection,),
        own_shape,
    )
    residual_q = input_q + scatter_head(grid, keep, give)
    mid_q = layer_norm(residual_q, mid_scales)
    mid_head = gather_head(grid, mid_q)
    mid_own = own_rows(mid_head)
    mid_pair = jnp.concatenate([part.reshape(-1, width) for part in mid_head[: grid.x]])
    mid_all = gather_along_seq(grid, mid_pair)
    cot_own = jnp.concatenate(
        [lax.dynamic_slice_in_dim(cotangent, quarters[i] * rows, rows, 1).reshape(-1, width) for i in range(grid.h)]
    )

    gate_pre = matmul(mid_own, gelu_weight)
    linear_pre = matmul(mid_own, linear_weight)
    hidden_own = gelu_gate(gate_pre, linear_pre).astype(BF)
    hidden_back = matmul(cot_own, down_weight.T)
    _, gelu_pull = jax.vjp(gelu_gate, gate_pre, linear_pre)
    gate_back, linear_back = (g.astype(BF) for g in gelu_pull(hidden_back))

    def halves(tall):
        split = tall.reshape(grid.c, *own_shape)
        return split[0], split[1]

    mid_part = matmul(gate_back, gelu_weight.T) + matmul(linear_back, linear_weight.T)
    mid_back = scatter_head(grid, *halves(mid_part))
    _, mid_pull = jax.vjp(layer_norm, residual_q, mid_scales)
    residual_back, mid_term = mid_pull(mid_back)
    residual_grad = cot_q + residual_back

    retained, carried, _ = retention_forward(order, forward_tables, rotated_query, rotated_key, values, edge)
    arrays, state = None, [no_state]
    for k in chunk_order(grid.z):
        pieces = gather_pieces(grid, residual_grad, k)
        near = slice(k * grid.y, (k + 1) * grid.y)
        arrays, state = chunk_call(
            lambda *refs: ungate_body(heads, seqs, *refs),
            (core, col),
            [*pieces, projection, retained, swish_pre, rotated_query, after, weigh_later[:, near]],
            [
                *[ANY] * 9,
                chunk_block((heads, chunk_rows, DV), k),
                chunk_block((heads, chunk_rows, DV), k),
                chunk_block((heads, chunk_rows, DK), k),
                full(after.shape),
                SMEM,
            ],
            [*[((heads, chunk_rows, DV), BF)] * 4, ((chunk_rows, mine), BF)],
            arrays,
            state,
            [
                piece_buffer(pieces[0]),
                pltpu.VMEM(projection.shape, BF),
                pltpu.VMEM((chunk_rows, width), BF),
                pltpu.VMEM((chunk_rows, DV), WIDE),
                pltpu.SemaphoreType.DMA((9,)),
            ],
            k,
            grid.z,
        )
    swish_back, ret_back, weighted_back, gated_out, back_slice = arrays
    later = state[0]
    backward_tables = (cosine, sine, within, after, before, through)
    path = order[::-1]
    token_args = (rotated_query, rotated_key, values, ret_back, weighted_back, swish_back, gated_out)
    edge = no_state
    if grid.groups > 1:
        *_, sums = retention_backward(path, backward_tables, token_args, (normed_slice, back_slice), carried, no_state)
        edge, here = outside(sums, True)
        later = later + here

    keep, give = own_call(
        own_backward_body,
        tile,
        (cosine, sine, within, after, before),
        (rotated_query, rotated_key, values, ret_back, swish_back),
        (held, later),
        (query_weight, key_weight, value_weight.T, swish_weight.T),
        own_shape,
    )
    input_back = scatter_head(grid, keep, give)
    _, input_pull = jax.vjp(layer_norm, input_q, pre_scales)
    input_return, pre_term = input_pull(input_back)
    input_grad = place(places, gather_head(grid, residual_grad + input_return), WIDE)

    summed = scatter_head(grid, *halves(matmul(hidden_own, down_weight)))
    block_output = place(places, gather_head(grid, residual_q + summed), BF)

    query_grad, key_grad, value_grad, swish_grad, projection_grad, _ = retention_backward(
        path, backward_tables, token_args, (normed_slice, back_slice), carried, edge
    )

    sums = [jnp.zeros((mine, hidden_units), WIDE)] * 3
    path = chunk_order(grid.z)
    for k in path:
        weights = (gelu_weight.T, linear_weight.T, down_weight)
        sums = feed(col, mid_all[k], cot_all[k], weights, sums, k == path[-1])
    down_grad, gelu_grad, linear_grad = sums

    gains = grid.sum_all(jnp.stack([pre_term, mid_term]))
    gain_len = width // grid.n
    gains = lax.dynamic_slice_in_dim(gains, seq_at * gain_len, gain_len, 1)
    return (
        block_output,
        input_grad,
        gains[0],
        total(query_grad, 0),
        total(key_grad, 0),
        total(value_grad.T, 0),
        total(swish_grad.T, 0),
        total(projection_grad, 1),
        gains[1],
        total(gelu_grad.T, 0),
        total(linear_grad.T, 0),
        total(down_grad, 1),
    )


def chunk_order(z):
    return sorted(range(z), key=lambda k: (min(k, z - k), k))


def solution(mesh):
    in_specs = (
        P(None, "seq", None),
        P(),
        P(None, ("x", "core")),
        P(None, ("x", "core")),
        P(None, ("x", "core")),
        P(None, ("x", "core")),
        P(("x", "core"), None),
        P(),
        P(None, ("x", "core")),
        P(None, ("x", "core")),
        P(("x", "core"), None),
        P(None, "seq", None),
    )
    out_specs = (
        P(None, "seq", None),
        P(None, "seq", None),
        P("seq"),
        P("seq", ("x", "core")),
        P("seq", ("x", "core")),
        P("seq", ("x", "core")),
        P("seq", ("x", "core")),
        P(("x", "core"), "seq"),
        P("seq"),
        P("seq", ("x", "core")),
        P("seq", ("x", "core")),
        P(("x", "core"), "seq"),
    )

    def run(*arrays):
        tokens_here = arrays[0].shape[0] * arrays[0].shape[1] // mesh.shape["seq"]
        grid = Grid(mesh.shape, tokens_here, arrays[0].shape[2])

        def body(*shards):
            return on_device(grid, *shards)

        split = Mesh(mesh.devices.reshape(grid.n, grid.x, grid.c), ALL)
        step = jax.shard_map(body, mesh=split, in_specs=in_specs, out_specs=out_specs, check_vma=False)
        return step(*arrays)

    return run
```
